32 devices in a mesh: mode: 8 (over z, x), var: 4 (over y, core).
Axes of the slice: x: 2, y: 2, z: 4, core: 2. Of those that a mesh axis runs over, the one named last changes fastest.
Arguments:
- control: bfloat16 [1, 4, 8, 1024, 1024], P(None, 'var', 'mode'), may hold values from -6 to 6
- filters: bfloat16 [3, 1024, 1024], replicated, may hold values from -4 to 5
- weights: bfloat16 [4, 3, 1024, 1024], P('var'), may hold values from 0.29882812 to 3
- vertical: bfloat16 [4, 64, 8], replicated, may hold values from -2 to 2
- balance: bfloat16 [3, 64, 64], replicated, may hold values from -0.75 to 0.75
Outputs:
- increment: bfloat16 [1, 4, 64, 1024, 1024], P(None, 'var', 'mode')
The draws below stay inside these ranges and needn't reach their ends.
All inputs are finite; a program needn't handle non-finite values.
Results may differ from the reference program's by a relative error of at most 0.006.
Values may be sent and summed in bfloat16 or wider, within the bound.
A program may use at most 128 MiB of HBM per device.

```python
import math
import jax
import jax.numpy as jnp
from jax import lax

MEMBERS = 1
NX = 1024
LEV = 64
FILTERS = 3
MODES = 8
VARS = 4


def draw_filters(key, part):
    index = jnp.arange(NX, dtype=jnp.float32)
    gap = index[:, None] - index[None, :]
    dense_scale = 0.25 / jnp.sqrt(jnp.float32(NX))
    mats = []
    for k, ratio in enumerate([128, 32, 8]):
        spread = NX / ratio
        envelope = jnp.exp(-(gap * gap) / (2.0 * spread * spread))
        scale_term = 1.0 / jnp.sqrt(spread * 1.7724539)
        sub = jax.random.fold_in(key, 11 + k)
        far_key = jax.random.fold_in(key, 31 + k)
        noise = jnp.clip(jax.random.normal(sub, (NX, NX), jnp.float32), -4.0, 4.0)
        dense = jnp.clip(jax.random.normal(far_key, (NX, NX), jnp.float32), -4.0, 4.0)
        mats.append(jnp.eye(NX, dtype=jnp.float32) + scale_term * envelope * noise + dense_scale * dense)
    return jnp.stack(mats).astype(jnp.bfloat16)


def block_levels(stream_key, shape, split, least, high):
    loudness = 1.0
    for axis_at, blocks in split:
        draws = jax.random.uniform(jax.random.fold_in(jax.random.fold_in(stream_key, 6), axis_at), (blocks,), jnp.float32, least / len(split), high / len(split))
        loudness = loudness * jnp.repeat(jnp.exp(draws), shape[axis_at] // blocks).reshape((-1,) + (1,) * (len(shape) - 1 - axis_at))
    return loudness


def centred(key, shape, scale, limit, split=(), kind=jnp.bfloat16):
    level = block_levels(key, shape, split, -0.22, 0.18) if split else 1.0
    drawn = jax.random.normal(key, shape, jnp.float32) * scale * level
    return jnp.minimum(jnp.maximum(drawn, -limit), limit).astype(kind)


def setup_inputs(seed: int = 0) -> dict:
    streams_of = jax.random.split(jax.random.key(seed), 6)
    return {
        "control": centred(streams_of[0], (MEMBERS, VARS, MODES, NX, NX), 1.0, 6.0, ((1, 4), (2, 8))),
        "filters": draw_filters(jax.random.fold_in(streams_of[5], 71), 0),
        "weights": jnp.clip(jnp.exp(math.log(3.0) - 2.306499 * jax.random.uniform(streams_of[2], (VARS, FILTERS, NX, NX), jnp.float32) ** block_levels(streams_of[2], (VARS, FILTERS, NX, NX), ((0, 4),), -0.2, 0.2)), 0.29882812, 3.0).astype(jnp.bfloat16),
        "vertical": centred(streams_of[3], (VARS, LEV, MODES), MODES ** -0.5, 2.0),
        "balance": centred(streams_of[4], (VARS - 1, LEV, LEV), LEV ** -0.5, 0.75),
    }


def smooth_plane(plane, filters, weights):
    total = jnp.zeros(plane.shape, jnp.float32)
    for k in range(FILTERS):
        half = jnp.dot(filters[k], plane, preferred_element_type=jnp.float32).astype(jnp.bfloat16)
        full = jnp.dot(half, filters[k].T, preferred_element_type=jnp.float32)
        total = total + weights[k].astype(jnp.float32) * full
    return total.astype(jnp.bfloat16)


def reference(control, filters, weights, vertical, balance):
    results = []
    for m in range(MEMBERS):
        filtered = []
        for v in range(VARS):
            planes = lax.map(lambda p: smooth_plane(p, filters, weights[v]), control[m, v])
            filtered.append(planes.reshape(MODES, NX * NX))
        stream_levels = jnp.dot(vertical[0], filtered[0], preferred_element_type=jnp.float32)
        stream = stream_levels.astype(jnp.bfloat16)
        outs = [stream]
        for v in range(1, VARS):
            levels = jnp.dot(vertical[v], filtered[v], preferred_element_type=jnp.float32)
            extra = jnp.dot(balance[v - 1], stream, preferred_element_type=jnp.float32)
            outs.append((levels + extra).astype(jnp.bfloat16))
        results.append(jnp.stack(outs).reshape(VARS, LEV, NX, NX))
    return jnp.stack(results)
```

```python
import functools

import jax
import jax.numpy as jnp
from jax import lax
from jax.experimental import pallas as pl
from jax.experimental.pallas import tpu as pltpu
from jax.sharding import PartitionSpec as P


def smooth(planes, filters, weights):
    total = jnp.zeros(planes.shape, jnp.float32)
    for k in range(filters.shape[0]):
        half = jnp.einsum(
            "ij,pjc->pic", filters[k], planes, preferred_element_type=jnp.float32
        ).astype(jnp.bfloat16)
        full = jnp.einsum("pic,dc->pid", half, filters[k], preferred_element_type=jnp.float32)
        total = total + weights[k].astype(jnp.float32) * full
    return total.astype(jnp.bfloat16)


def per_device_exchange(control, filters, weights, vertical, balance):
    members, _, depth, rows, cols = control.shape
    nmode = lax.axis_size("mode")
    nvar = lax.axis_size("var")
    strip = rows // (nmode * nvar)
    levcount = vertical.shape[1]
    filtered = smooth(control.reshape(members * depth, rows, cols), filters, weights[0])
    filtered = filtered.reshape(members, 1, depth, nvar, nmode, strip, cols)
    blocks = lax.all_to_all(
        lax.all_to_all(filtered, "mode", split_axis=4, concat_axis=2, tiled=True),
        "var",
        split_axis=3,
        concat_axis=1,
        tiled=True,
    )
    modecount = blocks.shape[2]
    blocks = blocks.reshape(members, nvar, modecount, strip * cols)
    levels = jnp.einsum("vlq,mvqc->mvlc", vertical, blocks, preferred_element_type=jnp.float32)
    stream = levels[:, 0].astype(jnp.bfloat16)
    extra = jnp.einsum("vlk,mkc->mvlc", balance, stream, preferred_element_type=jnp.float32)
    result = jnp.concatenate([levels[:, :1], levels[:, 1:] + extra], axis=1).astype(jnp.bfloat16)
    result = result.reshape(members, nvar, levcount, 1, 1, strip, cols)
    back = lax.all_to_all(
        lax.all_to_all(result, "mode", split_axis=2, concat_axis=4, tiled=True),
        "var",
        split_axis=1,
        concat_axis=3,
        tiled=True,
    )
    return back.reshape(members, 1, levcount // nmode, rows, cols)


GROUP = 16
LINE = 2
PAIRS = 4
CROSS = 8
EARLY = 6
LAG = 4


def fill_coefficients(mode, var, levels, nmode, vertical, balance, coef):
    height, width = levels * GROUP, nmode * GROUP
    levcount = vertical.shape[2]
    row = lax.broadcasted_iota(jnp.int32, (height, levcount), 0)
    col = lax.broadcasted_iota(jnp.int32, (height, levcount), 1)
    pick = (row // GROUP + mode * levels == col).astype(jnp.bfloat16)
    planes = lax.broadcasted_iota(jnp.int32, (nmode, width), 0)
    place = lax.broadcasted_iota(jnp.int32, (nmode, width), 1)
    spread = (planes == place // GROUP).astype(jnp.bfloat16)
    row = lax.broadcasted_iota(jnp.int32, (height, width), 0)
    col = lax.broadcasted_iota(jnp.int32, (height, width), 1)
    same = row % GROUP == col % GROUP

    def product(a, b, dims):
        return lax.dot_general(a, b, (dims, ((), ())), preferred_element_type=jnp.float32)

    def expand(values):
        wide = product(values.astype(jnp.bfloat16), spread, ((1,), (0,)))
        return jnp.where(same, wide, 0.0).astype(jnp.bfloat16)

    own = product(pick, vertical[var], ((1,), (1,)))
    regress = product(pick, balance[jnp.maximum(var - 1, 0)], ((1,), (0,)))
    folded = product(regress.astype(jnp.bfloat16), vertical[0], ((1,), (1,)))
    high = folded.astype(jnp.bfloat16)
    coef[:height, :width] = expand(own)
    coef[:height, width:] = expand(high)
    coef[height:, :width] = jnp.zeros((height, width), jnp.bfloat16)
    coef[height:, width:] = expand(folded - high.astype(jnp.float32))


def gather_kernel(
    nmode, nvar, chunks, control_in, filters_in, weights_in, vertical, balance, out,
    buf, coef, recv, own_send, up_send, down_send, turn_send, side_send, core_send,
    over_send, pair_send, in_sem,
):
    mode, var = lax.axis_index("mode"), lax.axis_index("var")
    z, x = mode // LINE, mode % LINE
    nz = nmode // LINE
    levels, rows, cols = out.shape
    nfilter = filters_in.shape[0]
    strip = rows // chunks
    early = EARLY * chunks // 16
    filters = [out.at[k] for k in range(nfilter)]
    weights = [out.at[nfilter + k] for k in range(nfilter)]
    control = out.at[2 * nfilter]

    loads = [pltpu.make_async_copy(control_in, control, in_sem.at[0])]
    loads += [
        pltpu.make_async_copy(filters_in.at[k], filters[k], in_sem.at[2 * k + 1])
        for k in range(nfilter)
    ]
    fetches = [
        pltpu.make_async_copy(weights_in.at[k], weights[k], in_sem.at[2 * k + 2])
        for k in range(nfilter)
    ]
    loads[0].start()
    for k in range(nfilter):
        loads[k + 1].start()
        fetches[k].start()

    low, high = z > 0, z < nz - 1
    stream, landing = var == 0, var == 2
    even = var % 2 == 0
    side = (z * LINE + 1 - x, var)
    above, below = (mode + LINE, var), (mode - LINE, var)
    core = (mode, var + 1 - 2 * (var % 2))
    across = (mode, 2 - var)
    near = z + 1 - 2 * (z % 2)
    pair = (near * LINE + x, var)

    barrier = pltpu.get_barrier_semaphore()
    count = jnp.int32(0)
    for exists, device in (
        (low, below), (high, above), (var >= 0, side), (var >= 0, core), (even, across),
    ):
        @pl.when(exists)
        def _(device=device):
            pl.semaphore_signal(
                barrier, inc=1, device_id=device, device_id_type=pl.DeviceIdType.MESH
            )
        count += exists.astype(jnp.int32)

    fill_coefficients(mode, var, levels, nmode, vertical, balance, coef)
    pl.semaphore_wait(barrier, count)

    def part(slot, j):
        return buf.at[slot, pl.ds(pl.multiple_of(j * strip, strip), strip)]

    def send(source, slot, j, sem, device):
        pltpu.make_async_remote_copy(
            part(source, j), part(slot, j), sem, recv.at[slot, j],
            device_id=device, device_id_type=pl.DeviceIdType.MESH,
        ).start()

    def await_part(slot, j):
        pltpu.make_async_copy(part(slot, j), part(slot, j), recv.at[slot, j]).wait()

    def await_sent(strips, sem):
        done = buf.at[0, pl.ds(0, strips * strip)]
        pltpu.make_async_copy(done, done, sem).wait()

    def plane(turn):
        fold = jnp.minimum(z, nz - 1 - z)
        flipped = turn + fold - 2 * turn * fold
        at = jnp.where(turn < 2, flipped, turn)
        return jnp.where(z < nz // 2, at, nz - 1 - at)

    def crosses(j):
        return j % CROSS == CROSS // 2

    ncross = sum(1 for j in range(chunks) if j % CROSS == CROSS // 2)
    depth = min(2 * strip, rows)

    def compute(i):
        at = pl.ds(pl.multiple_of(i * depth, depth), depth)
        total = jnp.zeros((depth, cols), jnp.float32)
        for k in range(nfilter):
            @pl.when(i == 0)
            def _(k=k):
                if k == 0:
                    loads[0].wait()
                loads[k + 1].wait()

            half = jnp.dot(filters[k][at], control[...], preferred_element_type=jnp.float32)
            full = lax.dot_general(
                half.astype(jnp.bfloat16), filters[k][...], (((1,), (1,)), ((), ())),
                preferred_element_type=jnp.float32,
            )

            @pl.when(i == 0)
            def _(k=k):
                fetches[k].wait()

            total += weights[k][at].astype(jnp.float32) * full
        buf[mode, at] = total.astype(jnp.bfloat16)

    def send_own(j):
        send(mode, mode, j, own_send.at[2], side)

        @pl.when(high)
        def _():
            send(mode, mode, j, own_send.at[0], above)

        @pl.when(low)
        def _():
            send(mode, mode, j, own_send.at[1], below)

        @pl.when(stream)
        def _():
            send(mode, mode + nmode, j, over_send.at[2 * nz - 1], across)
            send(mode, mode + nmode, j, core_send.at[2 * nz - 1], core)

    def along(turn, j):
        @pl.when(z > turn)
        def _():
            slot = mode - (turn + 1) * LINE
            await_part(slot, j)

            @pl.when(high)
            def _():
                send(slot, slot, j, up_send.at[turn], above)

        @pl.when(z + turn < nz - 1)
        def _():
            slot = mode + (turn + 1) * LINE
            await_part(slot, j)

            @pl.when(low)
            def _():
                send(slot, slot, j, down_send.at[turn], below)

        slot = plane(turn + 1) * LINE + x

        @pl.when(jnp.logical_not(crosses(j)))
        def _():
            send(slot, slot, j, side_send.at[turn], side)

        @pl.when(stream)
        def _():
            send(slot, slot + nmode, j, core_send.at[2 * turn], core)

            @pl.when(jnp.logical_or(turn > 0, j < early))
            def _():
                send(slot, slot + nmode, j, over_send.at[2 * turn], across)

    def beside(turn, j):
        other = z * LINE + 1 - x
        slot = plane(turn) * LINE + 1 - x

        @pl.when(crosses(j))
        def _():
            @pl.when(turn == 0)
            def _():
                await_part(other, j)

            @pl.when(jnp.logical_and(turn > 0, z >= turn))
            def _():
                await_part(other - turn * LINE, j)

            @pl.when(jnp.logical_and(turn > 0, z + turn < nz))
            def _():
                await_part(other + turn * LINE, j)

            @pl.when(jnp.logical_and(high, z >= turn))
            def _():
                came = other - turn * LINE
                send(came, came, j, turn_send.at[0, turn], above)

            @pl.when(jnp.logical_and(low, z + turn < nz))
            def _():
                came = other + turn * LINE
                send(came, came, j, turn_send.at[1, turn], below)

        @pl.when(stream)
        def _():
            @pl.when(jnp.logical_not(crosses(j)))
            def _():
                await_part(slot, j)

            send(slot, slot + nmode, j, over_send.at[2 * turn + (turn < nz - 1)], across)
            send(slot, slot + nmode, j, core_send.at[2 * turn + (turn < nz - 1)], core)

    def pass_on(slot, j, sem):
        await_part(slot + nmode, j)
        send(slot + nmode, slot + nmode, j, sem, core)

    def land_own(j):
        pass_on(mode, j, core_send.at[2 * nz - 1])

        @pl.when(j >= early)
        def _():
            send(mode + nmode, mode + nmode, j, pair_send.at[0], pair)

    def land(turn, j):
        @pl.when(jnp.logical_and(turn < nz - 1, jnp.logical_or(turn > 0, j < early)))
        def _():
            pass_on(plane(turn + 1) * LINE + x, j, core_send.at[2 * turn])

        slot = plane(turn) * LINE + 1 - x
        pass_on(slot, j, core_send.at[2 * turn + (turn < nz - 1)])

    height = levels * GROUP

    def combine(j):
        @pl.when(jnp.logical_not(stream))
        def _():
            @pl.when(jnp.logical_not(crosses(j)))
            def _():
                for turn in range(nz):
                    await_part(turn * LINE + 1 - x, j)

        @pl.when(jnp.logical_not(even))
        def _():
            for q in range(nmode):
                await_part(q + nmode, j)

        def put(i, sums):
            out[:, group(i)] = sums.reshape(levels, GROUP, cols).astype(jnp.bfloat16)

        def group(i):
            return pl.ds(pl.multiple_of(j * strip + i * GROUP, GROUP), GROUP)

        @pl.when(stream)
        def _():
            @pl.loop(0, strip // GROUP)
            def _(i):
                planes = buf[:nmode, group(i)].reshape(nmode * GROUP, cols)
                put(i, jnp.dot(
                    coef[:height, : nmode * GROUP], planes, preferred_element_type=jnp.float32
                ))

        @pl.when(jnp.logical_not(stream))
        def _():
            @pl.loop(0, strip // GROUP)
            def _(i):
                planes = buf[:, group(i)].reshape(2 * nmode * GROUP, cols)
                sums = jnp.dot(coef[...], planes, preferred_element_type=jnp.float32)
                put(i, sums[:height] + sums[height:])

    def within(i, first, last):
        return jnp.logical_and(i >= first, i < last)

    behind = jnp.where(var < 2, 0, LAG)

    @pl.loop(0, nz * chunks + LAG + 1)
    def _(step):
        @pl.when(step < rows // depth)
        def _():
            compute(step)
            for j in range(depth // strip):
                send_own(step * (depth // strip) + j)

        at = step - 1

        @pl.when(within(at, 0, (nz - 1) * chunks))
        def _():
            along(at // chunks, at % chunks)

        @pl.when(within(at, 0, nz * chunks))
        def _():
            beside(at // chunks, at % chunks)

        @pl.when(landing)
        def _():
            @pl.when(within(at, 0, chunks))
            def _():
                land_own(at)

            @pl.when(within(at - LAG, 0, nz * chunks))
            def _():
                land((at - LAG) // chunks, (at - LAG) % chunks)

            @pl.when(within(at - 2 * chunks, early, chunks))
            def _():
                pass_on(near * LINE + x, at - 2 * chunks, pair_send.at[1])

        done = at - (nz - 1) * chunks - behind

        @pl.when(within(done, 0, chunks))
        def _():
            combine(done)

    await_sent(chunks, own_send.at[2])

    @pl.when(high)
    def _():
        await_sent(chunks, own_send.at[0])

    @pl.when(low)
    def _():
        await_sent(chunks, own_send.at[1])

    for turn in range(nz):
        @pl.when(jnp.logical_and(high, z >= turn))
        def _():
            await_sent(ncross, turn_send.at[0, turn])

        @pl.when(jnp.logical_and(low, z + turn < nz))
        def _():
            await_sent(ncross, turn_send.at[1, turn])

    for turn in range(nz - 1):
        @pl.when(jnp.logical_and(high, z > turn))
        def _():
            await_sent(chunks, up_send.at[turn])

        @pl.when(jnp.logical_and(low, z + turn < nz - 1))
        def _():
            await_sent(chunks, down_send.at[turn])

        await_sent(chunks - ncross, side_send.at[turn])

    @pl.when(even)
    def _():
        for i in range(2 * nz):
            if i > 0:
                await_sent(chunks, core_send.at[i])

        @pl.when(stream)
        def _():
            await_sent(chunks, core_send.at[0])
            await_sent(early, over_send.at[0])
            for i in range(1, 2 * nz):
                await_sent(chunks, over_send.at[i])

        @pl.when(landing)
        def _():
            await_sent(early, core_send.at[0])
            await_sent(chunks - early, pair_send.at[0])
            await_sent(chunks - early, pair_send.at[1])


def per_device_gather(control, filters, weights, vertical, balance):
    members, _, depth, rows, cols = control.shape
    nmode, nvar = lax.axis_size("mode"), lax.axis_size("var")
    levels = vertical.shape[1] // nmode
    nz = nmode // LINE
    chunks = max(rows // 64, 1)
    vmem = pl.BlockSpec(memory_space=pltpu.VMEM)
    dma = pltpu.SemaphoreType.DMA
    out = pl.pallas_call(
        functools.partial(gather_kernel, nmode, nvar, chunks),
        out_shape=pltpu.VMEM((levels, rows, cols), jnp.bfloat16),
        in_specs=[pl.BlockSpec(memory_space=pl.ANY)] * 3 + [vmem] * 2,
        out_specs=vmem,
        scratch_shapes=[
            pltpu.VMEM((2 * nmode, rows, cols), jnp.bfloat16),
            pltpu.VMEM((2 * levels * GROUP, 2 * nmode * GROUP), jnp.bfloat16),
            dma((2 * nmode, chunks)),
            dma((3,)),
            dma((nz - 1,)),
            dma((nz - 1,)),
            dma((2, nz)),
            dma((nz - 1,)),
            dma((2 * nz,)),
            dma((2 * nz,)),
            dma((2,)),
            dma((2 * filters.shape[0] + 1,)),
        ],
        compiler_params=pltpu.CompilerParams(
            collective_id=0, has_side_effects=True, vmem_limit_bytes=42 * 2**20
        ),
    )(
        control.reshape(rows, cols), filters, weights[0],
        jnp.transpose(vertical, (0, 2, 1)), balance,
    )
    return out.reshape(members, 1, levels, rows, cols)


def solution(mesh):
    in_specs = (P(None, "var", "mode", None, None), P(), P("var", None, None, None), P(), P())
    out_specs = P(None, "var", "mode", None, None)
    nmode, nvar = mesh.shape["mode"], mesh.shape["var"]

    def run(control, filters, weights, vertical, balance):
        members, _, modes, rows, cols = control.shape
        levels = vertical.shape[1] // nmode
        gather = members == 1 and modes == nmode and nmode == LINE * PAIRS and nvar == 4
        gather = gather and rows % (64 * 16) == 0 and levels > 2 * filters.shape[0]
        gather = gather and (2 * modes + levels) * rows * cols * 2 <= 48 * 2**20
        body = per_device_gather if gather else per_device_exchange
        return jax.shard_map(
            body, mesh=mesh, in_specs=in_specs, out_specs=out_specs, check_vma=False
        )(control, filters, weights, vertical, balance)

    return run
```

```python
import functools

import jax
import jax.numpy as jnp
from jax import lax
from jax.experimental import pallas as pl
from jax.experimental.pallas import tpu as pltpu
from jax.sharding import PartitionSpec as P


def smooth(planes, filters, weights):
    total = jnp.zeros(planes.shape, jnp.float32)
    for k in range(filters.shape[0]):
        half = jnp.einsum(
            "ij,pjc->pic", filters[k], planes, preferred_element_type=jnp.float32
        ).astype(jnp.bfloat16)
        full = jnp.einsum("pic,dc->pid", half, filters[k], preferred_element_type=jnp.float32)
        total = total + weights[k].astype(jnp.float32) * full
    return total.astype(jnp.bfloat16)


def per_device_exchange(control, filters, weights, vertical, balance):
    members, _, depth, rows, cols = control.shape
    nmode = lax.axis_size("mode")
    nvar = lax.axis_size("var")
    strip = rows // (nmode * nvar)
    levcount = vertical.shape[1]
    filtered = smooth(control.reshape(members * depth, rows, cols), filters, weights[0])
    filtered = filtered.reshape(members, 1, depth, nvar, nmode, strip, cols)
    blocks = lax.all_to_all(
        lax.all_to_all(filtered, "mode", split_axis=4, concat_axis=2, tiled=True),
        "var",
        split_axis=3,
        concat_axis=1,
        tiled=True,
    )
    modecount = blocks.shape[2]
    blocks = blocks.reshape(members, nvar, modecount, strip * cols)
    levels = jnp.einsum("vlq,mvqc->mvlc", vertical, blocks, preferred_element_type=jnp.float32)
    stream = levels[:, 0].astype(jnp.bfloat16)
    extra = jnp.einsum("vlk,mkc->mvlc", balance, stream, preferred_element_type=jnp.float32)
    result = jnp.concatenate([levels[:, :1], levels[:, 1:] + extra], axis=1).astype(jnp.bfloat16)
    result = result.reshape(members, nvar, levcount, 1, 1, strip, cols)
    back = lax.all_to_all(
        lax.all_to_all(result, "mode", split_axis=2, concat_axis=4, tiled=True),
        "var",
        split_axis=1,
        concat_axis=3,
        tiled=True,
    )
    return back.reshape(members, 1, levcount // nmode, rows, cols)


GROUP = 16
LINE = 2
PAIRS = 4
CROSS = 8
EARLY = 6
LAG = 2
BLOCK = 4
DELAY = 4


def fill_coefficients(mode, var, levels, nmode, vertical, balance, coef):
    height, width = levels * GROUP, nmode * GROUP
    levcount = vertical.shape[2]
    row = lax.broadcasted_iota(jnp.int32, (height, levcount), 0)
    col = lax.broadcasted_iota(jnp.int32, (height, levcount), 1)
    pick = (row // GROUP + mode * levels == col).astype(jnp.bfloat16)
    planes = lax.broadcasted_iota(jnp.int32, (nmode, width), 0)
    place = lax.broadcasted_iota(jnp.int32, (nmode, width), 1)
    spread = (planes == place // GROUP).astype(jnp.bfloat16)
    row = lax.broadcasted_iota(jnp.int32, (height, width), 0)
    col = lax.broadcasted_iota(jnp.int32, (height, width), 1)
    same = row % GROUP == col % GROUP

    def product(a, b, dims):
        return lax.dot_general(a, b, (dims, ((), ())), preferred_element_type=jnp.float32)

    def expand(values):
        wide = product(values.astype(jnp.bfloat16), spread, ((1,), (0,)))
        return jnp.where(same, wide, 0.0).astype(jnp.bfloat16)

    own = product(pick, vertical[var], ((1,), (1,)))
    regress = product(pick, balance[jnp.maximum(var - 1, 0)], ((1,), (0,)))
    folded = product(regress.astype(jnp.bfloat16), vertical[0], ((1,), (1,)))
    high = folded.astype(jnp.bfloat16)
    coef[:height, :width] = expand(own)
    coef[:height, width:] = expand(high)
    coef[height:, :width] = jnp.zeros((height, width), jnp.bfloat16)
    coef[height:, width:] = expand(folded - high.astype(jnp.float32))


def gather_kernel(
    nmode, nvar, chunks, control_in, filters_in, weights_in, vertical, balance, out,
    buf, coef, recv, own_send, up_send, down_send, turn_send, side_send, core_send,
    over_send, pair_send, in_sem,
):
    mode, var = lax.axis_index("mode"), lax.axis_index("var")
    z, x = mode // LINE, mode % LINE
    nz = nmode // LINE
    levels, rows, cols = out.shape
    nfilter = filters_in.shape[0]
    strip = rows // chunks
    early = EARLY * chunks // 16
    filters = [out.at[k] for k in range(nfilter)]
    weights = [out.at[nfilter + k] for k in range(nfilter)]
    control = out.at[2 * nfilter]

    loads = [pltpu.make_async_copy(control_in, control, in_sem.at[0, 0])]
    loads += [
        pltpu.make_async_copy(filters_in.at[k], filters[k], in_sem.at[k + 1, 0])
        for k in range(nfilter)
    ]
    depth = BLOCK * strip
    begin, rest = pl.ds(0, depth), pl.ds(depth, rows - depth)
    fetches = [
        [
            pltpu.make_async_copy(
                weights_in.at[k, part], weights[k].at[part], in_sem.at[nfilter + 1 + k, i]
            )
            for k in range(nfilter)
        ]
        for i, part in enumerate((begin, rest))
    ]
    for load in loads + fetches[0] + fetches[1]:
        load.start()

    low, high = z > 0, z < nz - 1
    stream, landing = var == 0, var == 2
    even = var % 2 == 0
    side = (z * LINE + 1 - x, var)
    above, below = (mode + LINE, var), (mode - LINE, var)
    core = (mode, var + 1 - 2 * (var % 2))
    across = (mode, 2 - var)
    near = z + 1 - 2 * (z % 2)
    pair = (near * LINE + x, var)

    barrier = pltpu.get_barrier_semaphore()
    count = jnp.int32(0)
    for exists, device in (
        (low, below), (high, above), (var >= 0, side), (var >= 0, core), (even, across),
    ):
        @pl.when(exists)
        def _(device=device):
            pl.semaphore_signal(
                barrier, inc=1, device_id=device, device_id_type=pl.DeviceIdType.MESH
            )
        count += exists.astype(jnp.int32)

    def part(slot, j):
        return buf.at[slot, pl.ds(pl.multiple_of(j * strip, strip), strip)]

    def send(source, slot, j, sem, device):
        pltpu.make_async_remote_copy(
            part(source, j), part(slot, j), sem, recv.at[slot, j],
            device_id=device, device_id_type=pl.DeviceIdType.MESH,
        ).start()

    def await_part(slot, j):
        pltpu.make_async_copy(part(slot, j), part(slot, j), recv.at[slot, j]).wait()

    def await_sent(strips, sem):
        done = buf.at[0, pl.ds(0, strips * strip)]
        pltpu.make_async_copy(done, done, sem).wait()

    def plane(turn):
        fold = jnp.minimum(z, nz - 1 - z)
        flipped = turn + fold - 2 * turn * fold
        at = jnp.where(turn < 2, flipped, turn)
        return jnp.where(z < nz // 2, at, nz - 1 - at)

    def crosses(j):
        return j % CROSS == CROSS - 1

    ncross = sum(1 for j in range(chunks) if j % CROSS == CROSS - 1)
    def compute(i):
        at = pl.ds(pl.multiple_of(i * depth, depth), depth)
        total = jnp.zeros((depth, cols), jnp.float32)
        for k in range(nfilter):
            @pl.when(i == 0)
            def _(k=k):
                if k == 0:
                    loads[0].wait()
                loads[k + 1].wait()

            half = jnp.dot(filters[k][at], control[...], preferred_element_type=jnp.float32)
            full = lax.dot_general(
                half.astype(jnp.bfloat16), filters[k][...], (((1,), (1,)), ((), ())),
                preferred_element_type=jnp.float32,
            )

            @pl.when(i == 0)
            def _(k=k):
                fetches[0][k].wait()

            @pl.when(i == 1)
            def _(k=k):
                fetches[1][k].wait()

            total += weights[k][at].astype(jnp.float32) * full
        buf[mode, at] = total.astype(jnp.bfloat16)

    def send_own(j):
        send(mode, mode, j, own_send.at[2], side)

        @pl.when(high)
        def _():
            send(mode, mode, j, own_send.at[0], above)

        @pl.when(low)
        def _():
            send(mode, mode, j, own_send.at[1], below)

        @pl.when(stream)
        def _():
            send(mode, mode + nmode, j, over_send.at[2 * nz - 1], across)
            send(mode, mode + nmode, j, core_send.at[2 * nz - 1], core)

    def along(turn, j):
        @pl.when(var == 1)
        def _():
            await_part(plane(turn + 1) * LINE + x + nmode, j)

        @pl.when(z > turn)
        def _():
            slot = mode - (turn + 1) * LINE
            await_part(slot, j)

            @pl.when(high)
            def _():
                send(slot, slot, j, up_send.at[turn], above)

        @pl.when(z + turn < nz - 1)
        def _():
            slot = mode + (turn + 1) * LINE
            await_part(slot, j)

            @pl.when(low)
            def _():
                send(slot, slot, j, down_send.at[turn], below)

        slot = plane(turn + 1) * LINE + x

        @pl.when(jnp.logical_not(crosses(j)))
        def _():
            send(slot, slot, j, side_send.at[turn], side)

        @pl.when(stream)
        def _():
            send(slot, slot + nmode, j, core_send.at[2 * turn], core)

            @pl.when(jnp.logical_or(turn > 0, j < early))
            def _():
                send(slot, slot + nmode, j, over_send.at[2 * turn], across)

    def beside(turn, j):
        other = z * LINE + 1 - x
        slot = plane(turn) * LINE + 1 - x

        @pl.when(crosses(j))
        def _():
            @pl.when(turn == 0)
            def _():
                await_part(other, j)

            @pl.when(jnp.logical_and(turn > 0, z >= turn))
            def _():
                await_part(other - turn * LINE, j)

            @pl.when(jnp.logical_and(turn > 0, z + turn < nz))
            def _():
                await_part(other + turn * LINE, j)

            @pl.when(jnp.logical_and(high, z >= turn))
            def _():
                came = other - turn * LINE
                send(came, came, j, turn_send.at[0, turn], above)

            @pl.when(jnp.logical_and(low, z + turn < nz))
            def _():
                came = other + turn * LINE
                send(came, came, j, turn_send.at[1, turn], below)

        @pl.when(stream)
        def _():
            @pl.when(jnp.logical_not(crosses(j)))
            def _():
                await_part(slot, j)

            send(slot, slot + nmode, j, over_send.at[2 * turn + (turn < nz - 1)], across)
            send(slot, slot + nmode, j, core_send.at[2 * turn + (turn < nz - 1)], core)

    def pass_on(slot, j, sem):
        await_part(slot + nmode, j)
        send(slot + nmode, slot + nmode, j, sem, core)

    def land_own(j):
        pass_on(mode, j, core_send.at[2 * nz - 1])

    def land(turn, j):
        @pl.when(jnp.logical_and(turn < nz - 1, jnp.logical_or(turn > 0, j < early)))
        def _():
            pass_on(plane(turn + 1) * LINE + x, j, core_send.at[2 * turn])

        slot = plane(turn) * LINE + 1 - x
        pass_on(slot, j, core_send.at[2 * turn + (turn < nz - 1)])

    height = levels * GROUP

    def combine(j):
        @pl.when(jnp.logical_not(stream))
        def _():
            @pl.when(jnp.logical_not(crosses(j)))
            def _():
                for turn in range(nz):
                    await_part(turn * LINE + 1 - x, j)

        @pl.when(jnp.logical_and(landing, j >= early))
        def _():
            pass_on(near * LINE + x, j, pair_send.at[1])

        @pl.when(var == 1)
        def _():
            await_part(mode + nmode, j)
            for turn in range(nz):
                await_part(turn * LINE + 1 - x + nmode, j)

        @pl.when(var == 3)
        def _():
            for q in range(nmode):
                await_part(q + nmode, j)

        def put(i, sums):
            out[:, group(i)] = sums.reshape(levels, GROUP, cols).astype(jnp.bfloat16)

        def group(i):
            return pl.ds(pl.multiple_of(j * strip + i * GROUP, GROUP), GROUP)

        @pl.when(stream)
        def _():
            @pl.loop(0, strip // GROUP, unroll=strip // GROUP)
            def _(i):
                planes = buf[:nmode, group(i)].reshape(nmode * GROUP, cols)
                put(i, jnp.dot(
                    coef[:height, : nmode * GROUP], planes, preferred_element_type=jnp.float32
                ))

        @pl.when(jnp.logical_not(stream))
        def _():
            @pl.loop(0, strip // GROUP, unroll=strip // GROUP)
            def _(i):
                planes = buf[:, group(i)].reshape(2 * nmode * GROUP, cols)
                sums = jnp.dot(coef[...], planes, preferred_element_type=jnp.float32)
                put(i, sums[:height] + sums[height:])

    def within(i, first, last):
        return jnp.logical_and(i >= first, i < last)

    behind = jnp.where(var < 2, 0, LAG)

    blocks = chunks // BLOCK

    @pl.loop(0, nz * chunks + LAG + blocks)
    def _(step):
        own = step - jnp.where(var == 1, DELAY, 0)

        @pl.when(within(own, 0, blocks))
        def _():
            compute(own)

            @pl.when(own == 0)
            def _():
                pl.semaphore_wait(barrier, count)

            for j in range(BLOCK):
                send_own(own * BLOCK + j)

        @pl.when(step == blocks)
        def _():
            fill_coefficients(mode, var, levels, nmode, vertical, balance, coef)

        at = step - blocks

        @pl.when(within(at, 0, (nz - 1) * chunks))
        def _():
            along(at // chunks, at % chunks)

        @pl.when(within(at, 0, nz * chunks))
        def _():
            beside(at // chunks, at % chunks)

        @pl.when(landing)
        def _():
            @pl.when(within(at, 0, chunks))
            def _():
                land_own(at)

            @pl.when(within(at - LAG, 0, nz * chunks))
            def _():
                land((at - LAG) // chunks, (at - LAG) % chunks)

            @pl.when(within(at - 2 * chunks, early, chunks))
            def _():
                send(mode + nmode, mode + nmode, at - 2 * chunks, pair_send.at[0], pair)

        done = at - (nz - 1) * chunks - behind

        @pl.when(within(done, 0, chunks))
        def _():
            combine(done)

    await_sent(chunks, own_send.at[2])

    @pl.when(high)
    def _():
        await_sent(chunks, own_send.at[0])

    @pl.when(low)
    def _():
        await_sent(chunks, own_send.at[1])

    for turn in range(nz):
        @pl.when(jnp.logical_and(high, z >= turn))
        def _():
            await_sent(ncross, turn_send.at[0, turn])

        @pl.when(jnp.logical_and(low, z + turn < nz))
        def _():
            await_sent(ncross, turn_send.at[1, turn])

    for turn in range(nz - 1):
        @pl.when(jnp.logical_and(high, z > turn))
        def _():
            await_sent(chunks, up_send.at[turn])

        @pl.when(jnp.logical_and(low, z + turn < nz - 1))
        def _():
            await_sent(chunks, down_send.at[turn])

        await_sent(chunks - ncross, side_send.at[turn])

    @pl.when(even)
    def _():
        for i in range(2 * nz):
            if i > 0:
                await_sent(chunks, core_send.at[i])

        @pl.when(stream)
        def _():
            await_sent(chunks, core_send.at[0])
            await_sent(early, over_send.at[0])
            for i in range(1, 2 * nz):
                await_sent(chunks, over_send.at[i])

        @pl.when(landing)
        def _():
            await_sent(early, core_send.at[0])
            await_sent(chunks - early, pair_send.at[0])
            await_sent(chunks - early, pair_send.at[1])


def per_device_gather(control, filters, weights, vertical, balance):
    members, _, depth, rows, cols = control.shape
    nmode, nvar = lax.axis_size("mode"), lax.axis_size("var")
    levels = vertical.shape[1] // nmode
    nz = nmode // LINE
    chunks = max(rows // 64, 1)
    vmem = pl.BlockSpec(memory_space=pltpu.VMEM)
    dma = pltpu.SemaphoreType.DMA
    out = pl.pallas_call(
        functools.partial(gather_kernel, nmode, nvar, chunks),
        out_shape=pltpu.VMEM((levels, rows, cols), jnp.bfloat16),
        in_specs=[pl.BlockSpec(memory_space=pl.ANY)] * 3 + [vmem] * 2,
        out_specs=vmem,
        scratch_shapes=[
            pltpu.VMEM((2 * nmode, rows, cols), jnp.bfloat16),
            pltpu.VMEM((2 * levels * GROUP, 2 * nmode * GROUP), jnp.bfloat16),
            dma((2 * nmode, chunks)),
            dma((3,)),
            dma((nz - 1,)),
            dma((nz - 1,)),
            dma((2, nz)),
            dma((nz - 1,)),
            dma((2 * nz,)),
            dma((2 * nz,)),
            dma((2,)),
            dma((2 * filters.shape[0] + 1, 2)),
        ],
        compiler_params=pltpu.CompilerParams(
            collective_id=0, has_side_effects=True, vmem_limit_bytes=42 * 2**20
        ),
    )(
        control.reshape(rows, cols), filters, weights[0],
        jnp.transpose(vertical, (0, 2, 1)), balance,
    )
    return out.reshape(members, 1, levels, rows, cols)


def solution(mesh):
    in_specs = (P(None, "var", "mode", None, None), P(), P("var", None, None, None), P(), P())
    out_specs = P(None, "var", "mode", None, None)
    nmode, nvar = mesh.shape["mode"], mesh.shape["var"]

    def run(control, filters, weights, vertical, balance):
        members, _, modes, rows, cols = control.shape
        levels = vertical.shape[1] // nmode
        gather = members == 1 and modes == nmode and nmode == LINE * PAIRS and nvar == 4
        gather = gather and rows % (64 * 16) == 0 and levels > 2 * filters.shape[0]
        gather = gather and (2 * modes + levels) * rows * cols * 2 <= 48 * 2**20
        body = per_device_gather if gather else per_device_exchange
        return jax.shard_map(
            body, mesh=mesh, in_specs=in_specs, out_specs=out_specs, check_vma=False
        )(control, filters, weights, vertical, balance)

    return run
```

```python
import functools

import jax
import jax.numpy as jnp
from jax import lax
from jax.experimental import pallas as pl
from jax.experimental.pallas import tpu as pltpu
from jax.sharding import PartitionSpec as P


def smooth(planes, filters, weights):
    total = jnp.zeros(planes.shape, jnp.float32)
    for k in range(filters.shape[0]):
        half = jnp.einsum(
            "ij,pjc->pic", filters[k], planes, preferred_element_type=jnp.float32
        ).astype(jnp.bfloat16)
        full = jnp.einsum("pic,dc->pid", half, filters[k], preferred_element_type=jnp.float32)
        total = total + weights[k].astype(jnp.float32) * full
    return total.astype(jnp.bfloat16)


def per_device_exchange(control, filters, weights, vertical, balance):
    members, _, depth, rows, cols = control.shape
    nmode = lax.axis_size("mode")
    nvar = lax.axis_size("var")
    strip = rows // (nmode * nvar)
    levcount = vertical.shape[1]
    filtered = smooth(control.reshape(members * depth, rows, cols), filters, weights[0])
    filtered = filtered.reshape(members, 1, depth, nvar, nmode, strip, cols)
    blocks = lax.all_to_all(
        lax.all_to_all(filtered, "mode", split_axis=4, concat_axis=2, tiled=True),
        "var",
        split_axis=3,
        concat_axis=1,
        tiled=True,
    )
    modecount = blocks.shape[2]
    blocks = blocks.reshape(members, nvar, modecount, strip * cols)
    levels = jnp.einsum("vlq,mvqc->mvlc", vertical, blocks, preferred_element_type=jnp.float32)
    stream = levels[:, 0].astype(jnp.bfloat16)
    extra = jnp.einsum("vlk,mkc->mvlc", balance, stream, preferred_element_type=jnp.float32)
    result = jnp.concatenate([levels[:, :1], levels[:, 1:] + extra], axis=1).astype(jnp.bfloat16)
    result = result.reshape(members, nvar, levcount, 1, 1, strip, cols)
    back = lax.all_to_all(
        lax.all_to_all(result, "mode", split_axis=2, concat_axis=4, tiled=True),
        "var",
        split_axis=1,
        concat_axis=3,
        tiled=True,
    )
    return back.reshape(members, 1, levcount // nmode, rows, cols)


GROUP = 16
STRIP = 64
LINE = 2
PAIRS = 4
CROSS = 8
EARLY = 3
LAG = 0
BLOCK = 4
DELAY = 4
AHEAD = 5


def fill_coefficients(mode, var, levels, nmode, vertical, balance, coef):
    height, width = levels * GROUP, nmode * GROUP
    levcount = vertical.shape[2]
    row = lax.broadcasted_iota(jnp.int32, (height, levcount), 0)
    col = lax.broadcasted_iota(jnp.int32, (height, levcount), 1)
    pick = (row // GROUP + mode * levels == col).astype(jnp.bfloat16)
    planes = lax.broadcasted_iota(jnp.int32, (nmode, width), 0)
    place = lax.broadcasted_iota(jnp.int32, (nmode, width), 1)
    spread = (planes == place // GROUP).astype(jnp.bfloat16)
    row = lax.broadcasted_iota(jnp.int32, (height, width), 0)
    col = lax.broadcasted_iota(jnp.int32, (height, width), 1)
    same = row % GROUP == col % GROUP

    def product(a, b, dims):
        return lax.dot_general(a, b, (dims, ((), ())), preferred_element_type=jnp.float32)

    def expand(values):
        wide = product(values.astype(jnp.bfloat16), spread, ((1,), (0,)))
        return jnp.where(same, wide, 0.0).astype(jnp.bfloat16)

    own = product(pick, vertical[var], ((1,), (1,)))
    regress = product(pick, balance[jnp.maximum(var - 1, 0)], ((1,), (0,)))
    folded = product(regress.astype(jnp.bfloat16), vertical[0], ((1,), (1,)))
    high = folded.astype(jnp.bfloat16)
    coef[:height, :width] = expand(own)
    coef[:height, width:] = expand(high)
    coef[height:, :width] = jnp.zeros((height, width), jnp.bfloat16)
    coef[height:, width:] = expand(folded - high.astype(jnp.float32))


def gather_kernel(
    nmode, nvar, chunks, control_in, filters_in, weights_in, vertical_in, balance_in, out,
    buf, coef, recv, own_send, up_send, down_send, turn_send, side_send, core_send,
    over_send, pair_send, in_sem, vertical, balance,
):
    mode, var = lax.axis_index("mode"), lax.axis_index("var")
    z, x = mode // LINE, mode % LINE
    nz = nmode // LINE
    levels, rows, cols = out.shape
    nfilter = filters_in.shape[0]
    strip = rows // chunks
    early = EARLY * chunks // 8
    filters = [out.at[k] for k in range(nfilter)]
    weights = [out.at[nfilter + k] for k in range(nfilter)]
    control = out.at[2 * nfilter]

    loads = [pltpu.make_async_copy(control_in, control, in_sem.at[0, 0])]
    loads += [
        pltpu.make_async_copy(filters_in.at[k], filters[k], in_sem.at[k + 1, 0])
        for k in range(nfilter)
    ]
    depth = BLOCK * strip
    begin, rest = pl.ds(0, depth), pl.ds(depth, rows - depth)
    fetches = [
        [
            pltpu.make_async_copy(
                weights_in.at[k, part], weights[k].at[part], in_sem.at[nfilter + 1 + k, i]
            )
            for k in range(nfilter)
        ]
        for i, part in enumerate((begin, rest))
    ]
    tables = [
        pltpu.make_async_copy(vertical_in, vertical, in_sem.at[2 * nfilter + 1, 0]),
        pltpu.make_async_copy(balance_in, balance, in_sem.at[2 * nfilter + 1, 1]),
    ]
    for load in loads + fetches[0] + fetches[1] + tables:
        load.start()

    low, high = z > 0, z < nz - 1
    stream, landing = var == 0, var == 2
    even = var % 2 == 0
    side = (z * LINE + 1 - x, var)
    above, below = (mode + LINE, var), (mode - LINE, var)
    core = (mode, var + 1 - 2 * (var % 2))
    across = (mode, 2 - var)
    near = z + 1 - 2 * (z % 2)
    pair = (near * LINE + x, var)

    barrier = pltpu.get_barrier_semaphore()
    count = jnp.int32(0)
    for exists, device in (
        (low, below), (high, above), (var >= 0, side), (var >= 0, core), (even, across),
    ):
        @pl.when(exists)
        def _(device=device):
            pl.semaphore_signal(
                barrier, inc=1, device_id=device, device_id_type=pl.DeviceIdType.MESH
            )
        count += exists.astype(jnp.int32)

    def part(slot, j):
        return buf.at[slot, pl.ds(pl.multiple_of(j * strip, strip), strip)]

    def send(source, slot, j, sem, device):
        pltpu.make_async_remote_copy(
            part(source, j), part(slot, j), sem, recv.at[slot, j],
            device_id=device, device_id_type=pl.DeviceIdType.MESH,
        ).start()

    def await_part(slot, j):
        pltpu.make_async_copy(part(slot, j), part(slot, j), recv.at[slot, j]).wait()

    def await_sent(strips, sem):
        done = buf.at[0, pl.ds(0, strips * strip)]
        pltpu.make_async_copy(done, done, sem).wait()

    def plane(turn):
        fold = jnp.minimum(z, nz - 1 - z)
        flipped = turn + fold - 2 * turn * fold
        at = jnp.where(turn < 2, flipped, turn)
        return jnp.where(z < nz // 2, at, nz - 1 - at)

    def crosses(j):
        return j % CROSS == CROSS - 1

    ncross = sum(1 for j in range(chunks) if j % CROSS == CROSS - 1)
    def compute(i):
        at = pl.ds(pl.multiple_of(i * depth, depth), depth)
        total = jnp.zeros((depth, cols), jnp.float32)
        for k in range(nfilter):
            @pl.when(i == 0)
            def _(k=k):
                if k == 0:
                    loads[0].wait()
                loads[k + 1].wait()

            half = jnp.dot(filters[k][at], control[...], preferred_element_type=jnp.float32)
            full = lax.dot_general(
                half.astype(jnp.bfloat16), filters[k][...], (((1,), (1,)), ((), ())),
                preferred_element_type=jnp.float32,
            )

            @pl.when(i == 0)
            def _(k=k):
                fetches[0][k].wait()

            @pl.when(i == 1)
            def _(k=k):
                fetches[1][k].wait()

            total += weights[k][at].astype(jnp.float32) * full
        buf[mode, at] = total.astype(jnp.bfloat16)

    def send_own(j):
        send(mode, mode, j, own_send.at[2], side)

        @pl.when(high)
        def _():
            send(mode, mode, j, own_send.at[0], above)

        @pl.when(low)
        def _():
            send(mode, mode, j, own_send.at[1], below)

        @pl.when(stream)
        def _():
            send(mode, mode + nmode, j, over_send.at[2 * nz - 1], across)
            send(mode, mode + nmode, j, core_send.at[2 * nz - 1], core)

    def along(turn, j):
        @pl.when(var == 1)
        def _():
            await_part(plane(turn + 1) * LINE + x + nmode, j)

        @pl.when(z > turn)
        def _():
            slot = mode - (turn + 1) * LINE
            await_part(slot, j)

            @pl.when(high)
            def _():
                send(slot, slot, j, up_send.at[turn], above)

        @pl.when(z + turn < nz - 1)
        def _():
            slot = mode + (turn + 1) * LINE
            await_part(slot, j)

            @pl.when(low)
            def _():
                send(slot, slot, j, down_send.at[turn], below)

        slot = plane(turn + 1) * LINE + x

        @pl.when(jnp.logical_not(crosses(j)))
        def _():
            send(slot, slot, j, side_send.at[turn], side)

        @pl.when(stream)
        def _():
            send(slot, slot + nmode, j, core_send.at[2 * turn], core)

            @pl.when(jnp.logical_or(turn > 0, j < early))
            def _():
                send(slot, slot + nmode, j, over_send.at[2 * turn], across)

    def beside(turn, j):
        other = z * LINE + 1 - x
        slot = plane(turn) * LINE + 1 - x

        @pl.when(crosses(j))
        def _():
            @pl.when(turn == 0)
            def _():
                await_part(other, j)

            @pl.when(jnp.logical_and(turn > 0, z >= turn))
            def _():
                await_part(other - turn * LINE, j)

            @pl.when(jnp.logical_and(turn > 0, z + turn < nz))
            def _():
                await_part(other + turn * LINE, j)

            @pl.when(jnp.logical_and(high, z >= turn))
            def _():
                came = other - turn * LINE
                send(came, came, j, turn_send.at[0, turn], above)

            @pl.when(jnp.logical_and(low, z + turn < nz))
            def _():
                came = other + turn * LINE
                send(came, came, j, turn_send.at[1, turn], below)

        @pl.when(stream)
        def _():
            @pl.when(jnp.logical_not(crosses(j)))
            def _():
                await_part(slot, j)

            send(slot, slot + nmode, j, over_send.at[2 * turn + (turn < nz - 1)], across)
            send(slot, slot + nmode, j, core_send.at[2 * turn + (turn < nz - 1)], core)

    def pass_on(slot, j, sem):
        await_part(slot + nmode, j)
        send(slot + nmode, slot + nmode, j, sem, core)

    def land_own(j):
        pass_on(mode, j, core_send.at[2 * nz - 1])

    def land_along(turn, j):
        @pl.when(jnp.logical_or(turn > 0, j < early))
        def _():
            pass_on(plane(turn + 1) * LINE + x, j, core_send.at[2 * turn])

    def land_beside(turn, j):
        slot = plane(turn) * LINE + 1 - x
        pass_on(slot, j, core_send.at[2 * turn + (turn < nz - 1)])

    height = levels * GROUP

    def combine(j):
        @pl.when(jnp.logical_not(stream))
        def _():
            @pl.when(jnp.logical_not(crosses(j)))
            def _():
                for turn in range(nz):
                    await_part(turn * LINE + 1 - x, j)

        @pl.when(jnp.logical_and(landing, j >= early))
        def _():
            pass_on(near * LINE + x, j, pair_send.at[1])

        @pl.when(var == 1)
        def _():
            await_part(mode + nmode, j)
            for turn in range(nz):
                await_part(turn * LINE + 1 - x + nmode, j)

        @pl.when(var == 3)
        def _():
            for q in range(nmode):
                await_part(q + nmode, j)

        def put(i, sums):
            out[:, group(i)] = sums.reshape(levels, GROUP, cols).astype(jnp.bfloat16)

        def group(i):
            return pl.ds(pl.multiple_of(j * strip + i * GROUP, GROUP), GROUP)

        @pl.when(stream)
        def _():
            @pl.loop(0, strip // GROUP, unroll=4)
            def _(i):
                planes = buf[:nmode, group(i)].reshape(nmode * GROUP, cols)
                put(i, jnp.dot(
                    coef[:height, : nmode * GROUP], planes, preferred_element_type=jnp.float32
                ))

        @pl.when(jnp.logical_not(stream))
        def _():
            @pl.loop(0, strip // GROUP, unroll=4)
            def _(i):
                planes = buf[:, group(i)].reshape(2 * nmode * GROUP, cols)
                sums = jnp.dot(coef[...], planes, preferred_element_type=jnp.float32)
                put(i, sums[:height] + sums[height:])

    def within(i, first, last):
        return jnp.logical_and(i >= first, i < last)

    behind = jnp.where(var < 2, 0, LAG)

    blocks = chunks // BLOCK

    turns = nz * chunks
    steps = next(n for n in range(turns + 1) if n + n // AHEAD >= turns)

    def reach(at):
        return jnp.minimum(at + at // AHEAD, turns)

    def each(at, do):
        @pl.when(at >= 0)
        def _():
            @pl.loop(reach(at), reach(at + 1))
            def _(i):
                do(i // chunks, i % chunks)

    def finish(turn, j):
        @pl.when(turn == nz - 1)
        def _():
            combine(j)

    @pl.loop(0, blocks + steps + LAG)
    def _(step):
        own = step - jnp.where(var == 1, DELAY, 0)

        @pl.when(within(own, 0, blocks))
        def _():
            compute(own)

            @pl.when(own == 0)
            def _():
                pl.semaphore_wait(barrier, count)

            for j in range(BLOCK):
                send_own(own * BLOCK + j)

        @pl.when(step == blocks)
        def _():
            for table in tables:
                table.wait()
            fill_coefficients(mode, var, levels, nmode, vertical, balance, coef)

        at = step - blocks

        @pl.when(within(at, 0, (nz - 1) * chunks))
        def _():
            along(at // chunks, at % chunks)

        each(at, beside)

        @pl.when(landing)
        def _():
            @pl.when(within(at, 0, chunks))
            def _():
                land_own(at)

            @pl.when(within(at - LAG, 0, (nz - 1) * chunks))
            def _():
                land_along((at - LAG) // chunks, (at - LAG) % chunks)

            each(at - LAG, land_beside)

            @pl.when(within(at - 2 * chunks, early, chunks))
            def _():
                send(mode + nmode, mode + nmode, at - 2 * chunks, pair_send.at[0], pair)

        each(at - behind, finish)

    await_sent(chunks, own_send.at[2])

    @pl.when(high)
    def _():
        await_sent(chunks, own_send.at[0])

    @pl.when(low)
    def _():
        await_sent(chunks, own_send.at[1])

    for turn in range(nz):
        @pl.when(jnp.logical_and(high, z >= turn))
        def _():
            await_sent(ncross, turn_send.at[0, turn])

        @pl.when(jnp.logical_and(low, z + turn < nz))
        def _():
            await_sent(ncross, turn_send.at[1, turn])

    for turn in range(nz - 1):
        @pl.when(jnp.logical_and(high, z > turn))
        def _():
            await_sent(chunks, up_send.at[turn])

        @pl.when(jnp.logical_and(low, z + turn < nz - 1))
        def _():
            await_sent(chunks, down_send.at[turn])

        await_sent(chunks - ncross, side_send.at[turn])

    @pl.when(even)
    def _():
        for i in range(2 * nz):
            if i > 0:
                await_sent(chunks, core_send.at[i])

        @pl.when(stream)
        def _():
            await_sent(chunks, core_send.at[0])
            await_sent(early, over_send.at[0])
            for i in range(1, 2 * nz):
                await_sent(chunks, over_send.at[i])

        @pl.when(landing)
        def _():
            await_sent(early, core_send.at[0])
            await_sent(chunks - early, pair_send.at[0])
            await_sent(chunks - early, pair_send.at[1])


def per_device_gather(control, filters, weights, vertical, balance):
    members, _, depth, rows, cols = control.shape
    nmode, nvar = lax.axis_size("mode"), lax.axis_size("var")
    levels = vertical.shape[1] // nmode
    nz = nmode // LINE
    chunks = rows // STRIP
    vmem = pl.BlockSpec(memory_space=pltpu.VMEM)
    dma = pltpu.SemaphoreType.DMA
    out = pl.pallas_call(
        functools.partial(gather_kernel, nmode, nvar, chunks),
        out_shape=pltpu.VMEM((levels, rows, cols), jnp.bfloat16),
        in_specs=[pl.BlockSpec(memory_space=pl.ANY)] * 5,
        out_specs=vmem,
        scratch_shapes=[
            pltpu.VMEM((2 * nmode, rows, cols), jnp.bfloat16),
            pltpu.VMEM((2 * levels * GROUP, 2 * nmode * GROUP), jnp.bfloat16),
            dma((2 * nmode, chunks)),
            dma((3,)),
            dma((nz - 1,)),
            dma((nz - 1,)),
            dma((2, nz)),
            dma((nz - 1,)),
            dma((2 * nz,)),
            dma((2 * nz,)),
            dma((2,)),
            dma((2 * filters.shape[0] + 2, 2)),
            pltpu.VMEM(vertical.shape[:1] + vertical.shape[:0:-1], jnp.bfloat16),
            pltpu.VMEM(balance.shape, jnp.bfloat16),
        ],
        compiler_params=pltpu.CompilerParams(
            collective_id=0, has_side_effects=True, vmem_limit_bytes=42 * 2**20
        ),
    )(
        control.reshape(rows, cols), filters, weights[0],
        jnp.transpose(vertical, (0, 2, 1)), balance,
    )
    return out.reshape(members, 1, levels, rows, cols)


def solution(mesh):
    in_specs = (P(None, "var", "mode", None, None), P(), P("var", None, None, None), P(), P())
    out_specs = P(None, "var", "mode", None, None)
    nmode, nvar = mesh.shape["mode"], mesh.shape["var"]

    def run(control, filters, weights, vertical, balance):
        members, _, modes, rows, cols = control.shape
        levels = vertical.shape[1] // nmode
        gather = members == 1 and modes == nmode and nmode == LINE * PAIRS and nvar == 4
        gather = gather and rows % (8 * STRIP) == 0 and levels > 2 * filters.shape[0]
        gather = gather and (2 * modes + levels) * rows * cols * 2 <= 48 * 2**20
        body = per_device_gather if gather else per_device_exchange
        return jax.shard_map(
            body, mesh=mesh, in_specs=in_specs, out_specs=out_specs, check_vma=False
        )(control, filters, weights, vertical, balance)

    return run
```

```python
import functools

import jax
import jax.numpy as jnp
from jax import lax
from jax.experimental import pallas as pl
from jax.experimental.pallas import tpu as pltpu
from jax.sharding import PartitionSpec as P


def smooth(planes, filters, weights):
    total = jnp.zeros(planes.shape, jnp.float32)
    for k in range(filters.shape[0]):
        half = jnp.einsum(
            "ij,pjc->pic", filters[k], planes, preferred_element_type=jnp.float32
        ).astype(jnp.bfloat16)
        full = jnp.einsum("pic,dc->pid", half, filters[k], preferred_element_type=jnp.float32)
        total = total + weights[k].astype(jnp.float32) * full
    return total.astype(jnp.bfloat16)


def per_device_exchange(control, filters, weights, vertical, balance):
    members, _, depth, rows, cols = control.shape
    nmode = lax.axis_size("mode")
    nvar = lax.axis_size("var")
    strip = rows // (nmode * nvar)
    levcount = vertical.shape[1]
    filtered = smooth(control.reshape(members * depth, rows, cols), filters, weights[0])
    filtered = filtered.reshape(members, 1, depth, nvar, nmode, strip, cols)
    blocks = lax.all_to_all(
        lax.all_to_all(filtered, "mode", split_axis=4, concat_axis=2, tiled=True),
        "var",
        split_axis=3,
        concat_axis=1,
        tiled=True,
    )
    modecount = blocks.shape[2]
    blocks = blocks.reshape(members, nvar, modecount, strip * cols)
    levels = jnp.einsum("vlq,mvqc->mvlc", vertical, blocks, preferred_element_type=jnp.float32)
    stream = levels[:, 0].astype(jnp.bfloat16)
    extra = jnp.einsum("vlk,mkc->mvlc", balance, stream, preferred_element_type=jnp.float32)
    result = jnp.concatenate([levels[:, :1], levels[:, 1:] + extra], axis=1).astype(jnp.bfloat16)
    result = result.reshape(members, nvar, levcount, 1, 1, strip, cols)
    back = lax.all_to_all(
        lax.all_to_all(result, "mode", split_axis=2, concat_axis=4, tiled=True),
        "var",
        split_axis=1,
        concat_axis=3,
        tiled=True,
    )
    return back.reshape(members, 1, levcount // nmode, rows, cols)


GROUP = 16
STRIP = 64
LINE = 2
PAIRS = 4
CROSS = 8
EARLY = 3
LAG = 0
BLOCK = 4
DELAY = 4
AHEAD = 5


def fill_coefficients(mode, var, levels, nmode, vertical, balance, coef):
    height, width = levels * GROUP, nmode * GROUP
    levcount = vertical.shape[2]
    row = lax.broadcasted_iota(jnp.int32, (height, levcount), 0)
    col = lax.broadcasted_iota(jnp.int32, (height, levcount), 1)
    pick = (row // GROUP + mode * levels == col).astype(jnp.bfloat16)
    planes = lax.broadcasted_iota(jnp.int32, (nmode, width), 0)
    place = lax.broadcasted_iota(jnp.int32, (nmode, width), 1)
    spread = (planes == place // GROUP).astype(jnp.bfloat16)
    row = lax.broadcasted_iota(jnp.int32, (height, width), 0)
    col = lax.broadcasted_iota(jnp.int32, (height, width), 1)
    same = row % GROUP == col % GROUP

    def product(a, b, dims):
        return lax.dot_general(a, b, (dims, ((), ())), preferred_element_type=jnp.float32)

    def expand(values):
        wide = product(values.astype(jnp.bfloat16), spread, ((1,), (0,)))
        return jnp.where(same, wide, 0.0).astype(jnp.bfloat16)

    own = product(pick, vertical[var], ((1,), (1,)))
    regress = product(pick, balance[jnp.maximum(var - 1, 0)], ((1,), (0,)))
    folded = product(regress.astype(jnp.bfloat16), vertical[0], ((1,), (1,)))
    high = folded.astype(jnp.bfloat16)
    coef[:height, :width] = expand(own)
    coef[:height, width:] = expand(high)
    coef[height:, :width] = jnp.zeros((height, width), jnp.bfloat16)
    coef[height:, width:] = expand(folded - high.astype(jnp.float32))


def gather_kernel(
    nmode, nvar, chunks, control_in, filters_in, weights_in, vertical_in, balance_in, out,
    buf, coef, recv, own_send, up_send, down_send, turn_send, side_send, core_send,
    over_send, pair_send, in_sem, vertical, balance,
):
    mode, var = lax.axis_index("mode"), lax.axis_index("var")
    z, x = mode // LINE, mode % LINE
    nz = nmode // LINE
    levels, rows, cols = out.shape
    nfilter = filters_in.shape[0]
    strip = rows // chunks
    early = EARLY * chunks // 8
    filters = [out.at[k] for k in range(nfilter)]
    weights = [out.at[nfilter + k] for k in range(nfilter)]
    control = out.at[2 * nfilter]

    loads = [pltpu.make_async_copy(control_in, control, in_sem.at[0, 0])]
    loads += [
        pltpu.make_async_copy(filters_in.at[k], filters[k], in_sem.at[k + 1, 0])
        for k in range(nfilter)
    ]
    depth = BLOCK * strip
    begin, rest = pl.ds(0, depth), pl.ds(depth, rows - depth)
    fetches = [
        [
            pltpu.make_async_copy(
                weights_in.at[k, part], weights[k].at[part], in_sem.at[nfilter + 1 + k, i]
            )
            for k in range(nfilter)
        ]
        for i, part in enumerate((begin, rest))
    ]
    tables = [
        pltpu.make_async_copy(vertical_in, vertical, in_sem.at[2 * nfilter + 1, 0]),
        pltpu.make_async_copy(balance_in, balance, in_sem.at[2 * nfilter + 1, 1]),
    ]
    for load in loads + fetches[0] + fetches[1] + tables:
        load.start()

    low, high = z > 0, z < nz - 1
    stream, landing = var == 0, var == 2
    even = var % 2 == 0
    side = (z * LINE + 1 - x, var)
    above, below = (mode + LINE, var), (mode - LINE, var)
    core = (mode, var + 1 - 2 * (var % 2))
    across = (mode, 2 - var)
    near = z + 1 - 2 * (z % 2)
    pair = (near * LINE + x, var)

    barrier = pltpu.get_barrier_semaphore()
    count = jnp.int32(0)
    for exists, device in (
        (low, below), (high, above), (var >= 0, side), (var >= 0, core), (even, across),
    ):
        @pl.when(exists)
        def _(device=device):
            pl.semaphore_signal(
                barrier, inc=1, device_id=device, device_id_type=pl.DeviceIdType.MESH
            )
        count += exists.astype(jnp.int32)

    def part(slot, j):
        return buf.at[slot, pl.ds(pl.multiple_of(j * strip, strip), strip)]

    def send(source, slot, j, sem, device):
        pltpu.make_async_remote_copy(
            part(source, j), part(slot, j), sem, recv.at[slot, j],
            device_id=device, device_id_type=pl.DeviceIdType.MESH,
        ).start()

    def await_part(slot, j):
        pltpu.make_async_copy(part(slot, j), part(slot, j), recv.at[slot, j]).wait()

    def await_sent(strips, sem):
        done = buf.at[0, pl.ds(0, strips * strip)]
        pltpu.make_async_copy(done, done, sem).wait()

    def plane(turn):
        fold = jnp.minimum(z, nz - 1 - z)
        flipped = turn + fold - 2 * turn * fold
        at = jnp.where(turn < 2, flipped, turn)
        return jnp.where(z < nz // 2, at, nz - 1 - at)

    def crosses(j):
        return j % CROSS == CROSS - 1

    ncross = sum(1 for j in range(chunks) if j % CROSS == CROSS - 1)
    def compute(i):
        at = pl.ds(pl.multiple_of(i * depth, depth), depth)
        total = jnp.zeros((depth, cols), jnp.float32)
        for k in range(nfilter):
            @pl.when(i == 0)
            def _(k=k):
                if k == 0:
                    loads[0].wait()
                loads[k + 1].wait()

            half = jnp.dot(filters[k][at], control[...], preferred_element_type=jnp.float32)
            full = lax.dot_general(
                half.astype(jnp.bfloat16), filters[k][...], (((1,), (1,)), ((), ())),
                preferred_element_type=jnp.float32,
            )

            @pl.when(i == 0)
            def _(k=k):
                fetches[0][k].wait()

            @pl.when(i == 1)
            def _(k=k):
                fetches[1][k].wait()

            total += weights[k][at].astype(jnp.float32) * full
        buf[mode, at] = total.astype(jnp.bfloat16)

    def send_own(j):
        send(mode, mode, j, own_send.at[2], side)

        @pl.when(high)
        def _():
            send(mode, mode, j, own_send.at[0], above)

        @pl.when(low)
        def _():
            send(mode, mode, j, own_send.at[1], below)

        @pl.when(stream)
        def _():
            send(mode, mode + nmode, j, over_send.at[2 * nz - 1], across)
            send(mode, mode + nmode, j, core_send.at[2 * nz - 1], core)

    def along(turn, j):
        @pl.when(var == 1)
        def _():
            await_part(plane(turn + 1) * LINE + x + nmode, j)

        @pl.when(z > turn)
        def _():
            slot = mode - (turn + 1) * LINE
            await_part(slot, j)

            @pl.when(high)
            def _():
                send(slot, slot, j, up_send.at[turn], above)

        @pl.when(z + turn < nz - 1)
        def _():
            slot = mode + (turn + 1) * LINE
            await_part(slot, j)

            @pl.when(low)
            def _():
                send(slot, slot, j, down_send.at[turn], below)

        slot = plane(turn + 1) * LINE + x

        @pl.when(jnp.logical_not(crosses(j)))
        def _():
            send(slot, slot, j, side_send.at[turn], side)

        @pl.when(stream)
        def _():
            send(slot, slot + nmode, j, core_send.at[2 * turn], core)

            @pl.when(jnp.logical_or(turn > 0, j < early))
            def _():
                send(slot, slot + nmode, j, over_send.at[2 * turn], across)

    def beside(turn, j):
        other = z * LINE + 1 - x
        slot = plane(turn) * LINE + 1 - x

        @pl.when(crosses(j))
        def _():
            @pl.when(turn == 0)
            def _():
                await_part(other, j)

            @pl.when(jnp.logical_and(turn > 0, z >= turn))
            def _():
                await_part(other - turn * LINE, j)

            @pl.when(jnp.logical_and(turn > 0, z + turn < nz))
            def _():
                await_part(other + turn * LINE, j)

            @pl.when(jnp.logical_and(high, z >= turn))
            def _():
                came = other - turn * LINE
                send(came, came, j, turn_send.at[0, turn], above)

            @pl.when(jnp.logical_and(low, z + turn < nz))
            def _():
                came = other + turn * LINE
                send(came, came, j, turn_send.at[1, turn], below)

        @pl.when(stream)
        def _():
            @pl.when(jnp.logical_not(crosses(j)))
            def _():
                await_part(slot, j)

            send(slot, slot + nmode, j, over_send.at[2 * turn + (turn < nz - 1)], across)
            send(slot, slot + nmode, j, core_send.at[2 * turn + (turn < nz - 1)], core)

    def pass_on(slot, j, sem):
        await_part(slot + nmode, j)
        send(slot + nmode, slot + nmode, j, sem, core)

    def land_own(j):
        pass_on(mode, j, core_send.at[2 * nz - 1])

    def land_along(turn, j):
        @pl.when(jnp.logical_or(turn > 0, j < early))
        def _():
            pass_on(plane(turn + 1) * LINE + x, j, core_send.at[2 * turn])

    def land_beside(turn, j):
        slot = plane(turn) * LINE + 1 - x
        pass_on(slot, j, core_send.at[2 * turn + (turn < nz - 1)])

    height = levels * GROUP

    def combine(j):
        @pl.when(jnp.logical_not(stream))
        def _():
            @pl.when(jnp.logical_not(crosses(j)))
            def _():
                for turn in range(nz):
                    await_part(turn * LINE + 1 - x, j)

        @pl.when(jnp.logical_and(landing, j >= early))
        def _():
            pass_on(near * LINE + x, j, pair_send.at[1])

        @pl.when(var == 1)
        def _():
            await_part(mode + nmode, j)
            for turn in range(nz):
                await_part(turn * LINE + 1 - x + nmode, j)

        @pl.when(var == 3)
        def _():
            for q in range(nmode):
                await_part(q + nmode, j)

        def put(i, sums):
            out[:, group(i)] = sums.reshape(levels, GROUP, cols).astype(jnp.bfloat16)

        def group(i):
            return pl.ds(pl.multiple_of(j * strip + i * GROUP, GROUP), GROUP)

        @pl.when(stream)
        def _():
            @pl.loop(0, strip // GROUP, unroll=4)
            def _(i):
                planes = buf[:nmode, group(i)].reshape(nmode * GROUP, cols)
                put(i, jnp.dot(
                    coef[:height, : nmode * GROUP], planes, preferred_element_type=jnp.float32
                ))

        @pl.when(jnp.logical_not(stream))
        def _():
            @pl.loop(0, strip // GROUP, unroll=4)
            def _(i):
                planes = buf[:, group(i)].reshape(2 * nmode * GROUP, cols)
                sums = jnp.dot(coef[...], planes, preferred_element_type=jnp.float32)
                put(i, sums[:height] + sums[height:])

    def within(i, first, last):
        return jnp.logical_and(i >= first, i < last)

    behind = jnp.where(var < 2, 0, LAG)

    blocks = chunks // BLOCK

    turns = nz * chunks
    steps = next(n for n in range(turns + 1) if n + n // AHEAD >= turns)

    def reach(at):
        return jnp.minimum(at + at // AHEAD, turns)

    def each(at, do):
        @pl.when(at >= 0)
        def _():
            @pl.loop(reach(at), reach(at + 1))
            def _(i):
                do(i // chunks, i % chunks)

    def finish(turn, j):
        @pl.when(turn == nz - 1)
        def _():
            combine(j)

    @pl.loop(0, blocks + steps + LAG)
    def _(step):
        own = step - jnp.where(var == 1, DELAY, 0)

        @pl.when(within(own, 0, blocks))
        def _():
            compute(own)

            @pl.when(own == 0)
            def _():
                pl.semaphore_wait(barrier, count)

            for j in range(BLOCK):
                send_own(own * BLOCK + j)

        @pl.when(step == blocks)
        def _():
            for table in tables:
                table.wait()
            fill_coefficients(mode, var, levels, nmode, vertical, balance, coef)

        at = step - blocks

        @pl.when(within(at, 0, (nz - 1) * chunks))
        def _():
            along(at // chunks, at % chunks)

        each(at, beside)

        @pl.when(landing)
        def _():
            @pl.when(within(at, 0, chunks))
            def _():
                land_own(at)

            @pl.when(within(at - LAG, 0, (nz - 1) * chunks))
            def _():
                land_along((at - LAG) // chunks, (at - LAG) % chunks)

            each(at - LAG, land_beside)

            @pl.when(within(at - 2 * chunks, early, chunks))
            def _():
                send(mode + nmode, mode + nmode, at - 2 * chunks, pair_send.at[0], pair)

        each(at - behind, finish)

    await_sent(chunks, own_send.at[2])

    @pl.when(high)
    def _():
        await_sent(chunks, own_send.at[0])

    @pl.when(low)
    def _():
        await_sent(chunks, own_send.at[1])

    for turn in range(nz):
        @pl.when(jnp.logical_and(high, z >= turn))
        def _():
            await_sent(ncross, turn_send.at[0, turn])

        @pl.when(jnp.logical_and(low, z + turn < nz))
        def _():
            await_sent(ncross, turn_send.at[1, turn])

    for turn in range(nz - 1):
        @pl.when(jnp.logical_and(high, z > turn))
        def _():
            await_sent(chunks, up_send.at[turn])

        @pl.when(jnp.logical_and(low, z + turn < nz - 1))
        def _():
            await_sent(chunks, down_send.at[turn])

        await_sent(chunks - ncross, side_send.at[turn])

    @pl.when(even)
    def _():
        for i in range(2 * nz):
            if i > 0:
                await_sent(chunks, core_send.at[i])

        @pl.when(stream)
        def _():
            await_sent(chunks, core_send.at[0])
            await_sent(early, over_send.at[0])
            for i in range(1, 2 * nz):
                await_sent(chunks, over_send.at[i])

        @pl.when(landing)
        def _():
            await_sent(early, core_send.at[0])
            await_sent(chunks - early, pair_send.at[0])
            await_sent(chunks - early, pair_send.at[1])


def write_kernel(result, out, sem):
    copies = [
        pltpu.make_async_copy(result.at[i], out.at[i], sem.at[i]) for i in range(out.shape[0])
    ]
    for copy in copies:
        copy.start()
    for copy in copies:
        copy.wait()


def per_device_gather(control, filters, weights, vertical, balance):
    members, _, depth, rows, cols = control.shape
    nmode, nvar = lax.axis_size("mode"), lax.axis_size("var")
    levels = vertical.shape[1] // nmode
    nz = nmode // LINE
    chunks = rows // STRIP
    vmem = pl.BlockSpec(memory_space=pltpu.VMEM)
    dma = pltpu.SemaphoreType.DMA
    out = pl.pallas_call(
        functools.partial(gather_kernel, nmode, nvar, chunks),
        out_shape=pltpu.VMEM((levels, rows, cols), jnp.bfloat16),
        in_specs=[pl.BlockSpec(memory_space=pl.ANY)] * 5,
        out_specs=vmem,
        scratch_shapes=[
            pltpu.VMEM((2 * nmode, rows, cols), jnp.bfloat16),
            pltpu.VMEM((2 * levels * GROUP, 2 * nmode * GROUP), jnp.bfloat16),
            dma((2 * nmode, chunks)),
            dma((3,)),
            dma((nz - 1,)),
            dma((nz - 1,)),
            dma((2, nz)),
            dma((nz - 1,)),
            dma((2 * nz,)),
            dma((2 * nz,)),
            dma((2,)),
            dma((2 * filters.shape[0] + 2, 2)),
            pltpu.VMEM(vertical.shape[:1] + vertical.shape[:0:-1], jnp.bfloat16),
            pltpu.VMEM(balance.shape, jnp.bfloat16),
        ],
        compiler_params=pltpu.CompilerParams(
            collective_id=0, has_side_effects=True, vmem_limit_bytes=42 * 2**20
        ),
    )(
        control.reshape(rows, cols), filters, weights[0],
        jnp.transpose(vertical, (0, 2, 1)), balance,
    )
    out = pl.pallas_call(
        write_kernel,
        out_shape=jax.ShapeDtypeStruct((levels, rows, cols), jnp.bfloat16),
        in_specs=[pl.BlockSpec(memory_space=pl.ANY)],
        out_specs=pl.BlockSpec(memory_space=pl.ANY),
        scratch_shapes=[dma((levels,))],
        compiler_params=pltpu.CompilerParams(vmem_limit_bytes=2**20),
    )(pltpu.with_memory_space_constraint(out, pltpu.VMEM))
    return out.reshape(members, 1, levels, rows, cols)


def solution(mesh):
    in_specs = (P(None, "var", "mode", None, None), P(), P("var", None, None, None), P(), P())
    out_specs = P(None, "var", "mode", None, None)
    nmode, nvar = mesh.shape["mode"], mesh.shape["var"]

    def run(control, filters, weights, vertical, balance):
        members, _, modes, rows, cols = control.shape
        levels = vertical.shape[1] // nmode
        gather = members == 1 and modes == nmode and nmode == LINE * PAIRS and nvar == 4
        gather = gather and rows % (8 * STRIP) == 0 and levels > 2 * filters.shape[0]
        gather = gather and (2 * modes + levels) * rows * cols * 2 <= 48 * 2**20
        body = per_device_gather if gather else per_device_exchange
        return jax.shard_map(
            body, mesh=mesh, in_specs=in_specs, out_specs=out_specs, check_vma=False
        )(control, filters, weights, vertical, balance)

    return run
```

```python
import functools

import jax
import jax.numpy as jnp
from jax import lax
from jax.experimental import pallas as pl
from jax.experimental.pallas import tpu as pltpu
from jax.sharding import PartitionSpec as P


def smooth(planes, filters, weights):
    total = jnp.zeros(planes.shape, jnp.float32)
    for k in range(filters.shape[0]):
        half = jnp.einsum(
            "ij,pjc->pic", filters[k], planes, preferred_element_type=jnp.float32
        ).astype(jnp.bfloat16)
        full = jnp.einsum("pic,dc->pid", half, filters[k], preferred_element_type=jnp.float32)
        total = total + weights[k].astype(jnp.float32) * full
    return total.astype(jnp.bfloat16)


def per_device_exchange(control, filters, weights, vertical, balance):
    members, _, depth, rows, cols = control.shape
    nmode = lax.axis_size("mode")
    nvar = lax.axis_size("var")
    strip = rows // (nmode * nvar)
    levcount = vertical.shape[1]
    filtered = smooth(control.reshape(members * depth, rows, cols), filters, weights[0])
    filtered = filtered.reshape(members, 1, depth, nvar, nmode, strip, cols)
    blocks = lax.all_to_all(
        lax.all_to_all(filtered, "mode", split_axis=4, concat_axis=2, tiled=True),
        "var",
        split_axis=3,
        concat_axis=1,
        tiled=True,
    )
    modecount = blocks.shape[2]
    blocks = blocks.reshape(members, nvar, modecount, strip * cols)
    levels = jnp.einsum("vlq,mvqc->mvlc", vertical, blocks, preferred_element_type=jnp.float32)
    stream = levels[:, 0].astype(jnp.bfloat16)
    extra = jnp.einsum("vlk,mkc->mvlc", balance, stream, preferred_element_type=jnp.float32)
    result = jnp.concatenate([levels[:, :1], levels[:, 1:] + extra], axis=1).astype(jnp.bfloat16)
    result = result.reshape(members, nvar, levcount, 1, 1, strip, cols)
    back = lax.all_to_all(
        lax.all_to_all(result, "mode", split_axis=2, concat_axis=4, tiled=True),
        "var",
        split_axis=1,
        concat_axis=3,
        tiled=True,
    )
    return back.reshape(members, 1, levcount // nmode, rows, cols)


GROUP = 16
STRIP = 64
LINE = 2
PAIRS = 4
CROSS = 8
EARLY = 3
LAG = 0
BLOCK = 4
DELAY = 4
AHEAD = 5
PARTS = 2


def fill_coefficients(mode, var, levels, nmode, vertical, balance, coef):
    height, width = levels * GROUP, nmode * GROUP
    levcount = vertical.shape[2]
    row = lax.broadcasted_iota(jnp.int32, (height, levcount), 0)
    col = lax.broadcasted_iota(jnp.int32, (height, levcount), 1)
    pick = (row // GROUP + mode * levels == col).astype(jnp.bfloat16)
    planes = lax.broadcasted_iota(jnp.int32, (nmode, width), 0)
    place = lax.broadcasted_iota(jnp.int32, (nmode, width), 1)
    spread = (planes == place // GROUP).astype(jnp.bfloat16)
    row = lax.broadcasted_iota(jnp.int32, (height, width), 0)
    col = lax.broadcasted_iota(jnp.int32, (height, width), 1)
    same = row % GROUP == col % GROUP

    def product(a, b, dims):
        return lax.dot_general(a, b, (dims, ((), ())), preferred_element_type=jnp.float32)

    def expand(values):
        wide = product(values.astype(jnp.bfloat16), spread, ((1,), (0,)))
        return jnp.where(same, wide, 0.0).astype(jnp.bfloat16)

    own = product(pick, vertical[var], ((1,), (1,)))
    regress = product(pick, balance[jnp.maximum(var - 1, 0)], ((1,), (0,)))
    folded = product(regress.astype(jnp.bfloat16), vertical[0], ((1,), (1,)))
    high = folded.astype(jnp.bfloat16)
    coef[:height, :width] = expand(own)
    coef[:height, width:] = expand(high)
    coef[height:, :width] = jnp.zeros((height, width), jnp.bfloat16)
    coef[height:, width:] = expand(folded - high.astype(jnp.float32))


def gather_kernel(
    nmode, nvar, chunks, control_in, filters_in, weights_in, vertical_in, balance_in, out,
    buf, coef, recv, own_send, up_send, down_send, turn_send, side_send, core_send,
    over_send, pair_send, in_sem, vertical, balance,
):
    mode, var = lax.axis_index("mode"), lax.axis_index("var")
    z, x = mode // LINE, mode % LINE
    nz = nmode // LINE
    levels, rows, cols = out.shape
    nfilter = filters_in.shape[0]
    strip = rows // chunks
    early = EARLY * chunks // 8
    filters = [out.at[k] for k in range(nfilter)]
    weights = [out.at[nfilter + k] for k in range(nfilter)]
    control = out.at[2 * nfilter]

    loads = [pltpu.make_async_copy(control_in, control, in_sem.at[0, 0])]
    loads += [
        pltpu.make_async_copy(filters_in.at[k], filters[k], in_sem.at[k + 1, 0])
        for k in range(nfilter)
    ]
    depth = BLOCK * strip
    begin, rest = pl.ds(0, depth), pl.ds(depth, rows - depth)
    fetches = [
        [
            pltpu.make_async_copy(
                weights_in.at[k, part], weights[k].at[part], in_sem.at[nfilter + 1 + k, i]
            )
            for k in range(nfilter)
        ]
        for i, part in enumerate((begin, rest))
    ]
    tables = [
        pltpu.make_async_copy(vertical_in, vertical, in_sem.at[2 * nfilter + 1, 0]),
        pltpu.make_async_copy(balance_in, balance, in_sem.at[2 * nfilter + 1, 1]),
    ]
    for load in loads + fetches[0] + fetches[1] + tables:
        load.start()

    low, high = z > 0, z < nz - 1
    stream, landing = var == 0, var == 2
    even = var % 2 == 0
    side = (z * LINE + 1 - x, var)
    above, below = (mode + LINE, var), (mode - LINE, var)
    core = (mode, var + 1 - 2 * (var % 2))
    across = (mode, 2 - var)
    near = z + 1 - 2 * (z % 2)
    pair = (near * LINE + x, var)

    barrier = pltpu.get_barrier_semaphore()
    count = jnp.int32(0)
    for exists, device in (
        (low, below), (high, above), (var >= 0, side), (var >= 0, core), (even, across),
    ):
        @pl.when(exists)
        def _(device=device):
            pl.semaphore_signal(
                barrier, inc=1, device_id=device, device_id_type=pl.DeviceIdType.MESH
            )
        count += exists.astype(jnp.int32)

    def part(slot, j):
        return buf.at[slot, pl.ds(pl.multiple_of(j * strip, strip), strip)]

    def send(source, slot, j, sem, device):
        pltpu.make_async_remote_copy(
            part(source, j), part(slot, j), sem, recv.at[slot, j],
            device_id=device, device_id_type=pl.DeviceIdType.MESH,
        ).start()

    def await_part(slot, j):
        pltpu.make_async_copy(part(slot, j), part(slot, j), recv.at[slot, j]).wait()

    def await_sent(strips, sem):
        done = buf.at[0, pl.ds(0, strips * strip)]
        pltpu.make_async_copy(done, done, sem).wait()

    def plane(turn):
        fold = jnp.minimum(z, nz - 1 - z)
        flipped = turn + fold - 2 * turn * fold
        at = jnp.where(turn < 2, flipped, turn)
        return jnp.where(z < nz // 2, at, nz - 1 - at)

    def crosses(j):
        return j % CROSS == CROSS - 1

    ncross = sum(1 for j in range(chunks) if j % CROSS == CROSS - 1)
    def compute(i):
        at = pl.ds(pl.multiple_of(i * depth, depth), depth)
        total = jnp.zeros((depth, cols), jnp.float32)
        for k in range(nfilter):
            @pl.when(i == 0)
            def _(k=k):
                if k == 0:
                    loads[0].wait()
                loads[k + 1].wait()

            half = jnp.dot(filters[k][at], control[...], preferred_element_type=jnp.float32)
            full = lax.dot_general(
                half.astype(jnp.bfloat16), filters[k][...], (((1,), (1,)), ((), ())),
                preferred_element_type=jnp.float32,
            )

            @pl.when(i == 0)
            def _(k=k):
                fetches[0][k].wait()

            @pl.when(i == 1)
            def _(k=k):
                fetches[1][k].wait()

            total += weights[k][at].astype(jnp.float32) * full
        buf[mode, at] = total.astype(jnp.bfloat16)

    def send_own(j):
        send(mode, mode, j, own_send.at[2], side)

        @pl.when(high)
        def _():
            send(mode, mode, j, own_send.at[0], above)

        @pl.when(low)
        def _():
            send(mode, mode, j, own_send.at[1], below)

        @pl.when(stream)
        def _():
            send(mode, mode + nmode, j, over_send.at[2 * nz - 1], across)
            send(mode, mode + nmode, j, core_send.at[2 * nz - 1], core)

    def along(turn, j):
        @pl.when(var == 1)
        def _():
            await_part(plane(turn + 1) * LINE + x + nmode, j)

        @pl.when(z > turn)
        def _():
            slot = mode - (turn + 1) * LINE
            await_part(slot, j)

            @pl.when(high)
            def _():
                send(slot, slot, j, up_send.at[turn], above)

        @pl.when(z + turn < nz - 1)
        def _():
            slot = mode + (turn + 1) * LINE
            await_part(slot, j)

            @pl.when(low)
            def _():
                send(slot, slot, j, down_send.at[turn], below)

        slot = plane(turn + 1) * LINE + x

        @pl.when(jnp.logical_not(crosses(j)))
        def _():
            send(slot, slot, j, side_send.at[turn], side)

        @pl.when(stream)
        def _():
            send(slot, slot + nmode, j, core_send.at[2 * turn], core)

            @pl.when(jnp.logical_or(turn > 0, j < early))
            def _():
                send(slot, slot + nmode, j, over_send.at[2 * turn], across)

    def beside(turn, j):
        other = z * LINE + 1 - x
        slot = plane(turn) * LINE + 1 - x

        @pl.when(crosses(j))
        def _():
            @pl.when(turn == 0)
            def _():
                await_part(other, j)

            @pl.when(jnp.logical_and(turn > 0, z >= turn))
            def _():
                await_part(other - turn * LINE, j)

            @pl.when(jnp.logical_and(turn > 0, z + turn < nz))
            def _():
                await_part(other + turn * LINE, j)

            @pl.when(jnp.logical_and(high, z >= turn))
            def _():
                came = other - turn * LINE
                send(came, came, j, turn_send.at[0, turn], above)

            @pl.when(jnp.logical_and(low, z + turn < nz))
            def _():
                came = other + turn * LINE
                send(came, came, j, turn_send.at[1, turn], below)

        @pl.when(stream)
        def _():
            @pl.when(jnp.logical_not(crosses(j)))
            def _():
                await_part(slot, j)

            send(slot, slot + nmode, j, over_send.at[2 * turn + (turn < nz - 1)], across)
            send(slot, slot + nmode, j, core_send.at[2 * turn + (turn < nz - 1)], core)

    def pass_on(slot, j, sem):
        await_part(slot + nmode, j)
        send(slot + nmode, slot + nmode, j, sem, core)

    def land_own(j):
        pass_on(mode, j, core_send.at[2 * nz - 1])

    def land_along(turn, j):
        @pl.when(jnp.logical_or(turn > 0, j < early))
        def _():
            pass_on(plane(turn + 1) * LINE + x, j, core_send.at[2 * turn])

    def land_beside(turn, j):
        slot = plane(turn) * LINE + 1 - x
        pass_on(slot, j, core_send.at[2 * turn + (turn < nz - 1)])

    height = levels * GROUP

    def combine(j):
        @pl.when(jnp.logical_not(stream))
        def _():
            @pl.when(jnp.logical_not(crosses(j)))
            def _():
                for turn in range(nz):
                    await_part(turn * LINE + 1 - x, j)

        @pl.when(jnp.logical_and(landing, j >= early))
        def _():
            pass_on(near * LINE + x, j, pair_send.at[1])

        @pl.when(var == 1)
        def _():
            await_part(mode + nmode, j)
            for turn in range(nz):
                await_part(turn * LINE + 1 - x + nmode, j)

        @pl.when(var == 3)
        def _():
            for q in range(nmode):
                await_part(q + nmode, j)

        def put(i, sums):
            out[:, group(i)] = sums.reshape(levels, GROUP, cols).astype(jnp.bfloat16)

        def group(i):
            return pl.ds(pl.multiple_of(j * strip + i * GROUP, GROUP), GROUP)

        @pl.when(stream)
        def _():
            @pl.loop(0, strip // GROUP, unroll=4)
            def _(i):
                planes = buf[:nmode, group(i)].reshape(nmode * GROUP, cols)
                put(i, jnp.dot(
                    coef[:height, : nmode * GROUP], planes, preferred_element_type=jnp.float32
                ))

        @pl.when(jnp.logical_not(stream))
        def _():
            @pl.loop(0, strip // GROUP, unroll=4)
            def _(i):
                planes = buf[:, group(i)].reshape(2 * nmode * GROUP, cols)
                sums = jnp.dot(coef[...], planes, preferred_element_type=jnp.float32)
                put(i, sums[:height] + sums[height:])

    def within(i, first, last):
        return jnp.logical_and(i >= first, i < last)

    behind = jnp.where(var < 2, 0, LAG)

    blocks = chunks // BLOCK

    turns = nz * chunks
    steps = next(n for n in range(turns + 1) if n + n // AHEAD >= turns)

    def reach(at):
        return jnp.minimum(at + at // AHEAD, turns)

    def each(at, do):
        @pl.when(at >= 0)
        def _():
            @pl.loop(reach(at), reach(at + 1))
            def _(i):
                do(i // chunks, i % chunks)

    def finish(turn, j):
        @pl.when(turn == nz - 1)
        def _():
            combine(j)

    @pl.loop(0, blocks + steps + LAG)
    def _(step):
        own = step - jnp.where(var == 1, DELAY, 0)

        @pl.when(within(own, 0, blocks))
        def _():
            compute(own)

            @pl.when(own == 0)
            def _():
                pl.semaphore_wait(barrier, count)

            for j in range(BLOCK):
                send_own(own * BLOCK + j)

        @pl.when(step == blocks)
        def _():
            for table in tables:
                table.wait()
            fill_coefficients(mode, var, levels, nmode, vertical, balance, coef)

        at = step - blocks

        @pl.when(within(at, 0, (nz - 1) * chunks))
        def _():
            along(at // chunks, at % chunks)

        each(at, beside)

        @pl.when(landing)
        def _():
            @pl.when(within(at, 0, chunks))
            def _():
                land_own(at)

            @pl.when(within(at - LAG, 0, (nz - 1) * chunks))
            def _():
                land_along((at - LAG) // chunks, (at - LAG) % chunks)

            each(at - LAG, land_beside)

            @pl.when(within(at - 2 * chunks, early, chunks))
            def _():
                send(mode + nmode, mode + nmode, at - 2 * chunks, pair_send.at[0], pair)

        each(at - behind, finish)

    await_sent(chunks, own_send.at[2])

    @pl.when(high)
    def _():
        await_sent(chunks, own_send.at[0])

    @pl.when(low)
    def _():
        await_sent(chunks, own_send.at[1])

    for turn in range(nz):
        @pl.when(jnp.logical_and(high, z >= turn))
        def _():
            await_sent(ncross, turn_send.at[0, turn])

        @pl.when(jnp.logical_and(low, z + turn < nz))
        def _():
            await_sent(ncross, turn_send.at[1, turn])

    for turn in range(nz - 1):
        @pl.when(jnp.logical_and(high, z > turn))
        def _():
            await_sent(chunks, up_send.at[turn])

        @pl.when(jnp.logical_and(low, z + turn < nz - 1))
        def _():
            await_sent(chunks, down_send.at[turn])

        await_sent(chunks - ncross, side_send.at[turn])

    @pl.when(even)
    def _():
        for i in range(2 * nz):
            if i > 0:
                await_sent(chunks, core_send.at[i])

        @pl.when(stream)
        def _():
            await_sent(chunks, core_send.at[0])
            await_sent(early, over_send.at[0])
            for i in range(1, 2 * nz):
                await_sent(chunks, over_send.at[i])

        @pl.when(landing)
        def _():
            await_sent(early, core_send.at[0])
            await_sent(chunks - early, pair_send.at[0])
            await_sent(chunks - early, pair_send.at[1])


def write_kernel(result, out, sem):
    size = out.shape[1] // PARTS
    parts = [pl.ds(n * size, size) for n in range(PARTS)]
    copies = [
        pltpu.make_async_copy(result.at[i, part], out.at[i, part], sem.at[i, n])
        for i in range(out.shape[0])
        for n, part in enumerate(parts)
    ]
    for copy in copies:
        copy.start()
    for copy in copies:
        copy.wait()


def per_device_gather(control, filters, weights, vertical, balance):
    members, _, depth, rows, cols = control.shape
    nmode, nvar = lax.axis_size("mode"), lax.axis_size("var")
    levels = vertical.shape[1] // nmode
    nz = nmode // LINE
    chunks = rows // STRIP
    vmem = pl.BlockSpec(memory_space=pltpu.VMEM)
    dma = pltpu.SemaphoreType.DMA
    out = pl.pallas_call(
        functools.partial(gather_kernel, nmode, nvar, chunks),
        out_shape=pltpu.VMEM((levels, rows, cols), jnp.bfloat16),
        in_specs=[pl.BlockSpec(memory_space=pl.ANY)] * 5,
        out_specs=vmem,
        scratch_shapes=[
            pltpu.VMEM((2 * nmode, rows, cols), jnp.bfloat16),
            pltpu.VMEM((2 * levels * GROUP, 2 * nmode * GROUP), jnp.bfloat16),
            dma((2 * nmode, chunks)),
            dma((3,)),
            dma((nz - 1,)),
            dma((nz - 1,)),
            dma((2, nz)),
            dma((nz - 1,)),
            dma((2 * nz,)),
            dma((2 * nz,)),
            dma((2,)),
            dma((2 * filters.shape[0] + 2, 2)),
            pltpu.VMEM(vertical.shape[:1] + vertical.shape[:0:-1], jnp.bfloat16),
            pltpu.VMEM(balance.shape, jnp.bfloat16),
        ],
        compiler_params=pltpu.CompilerParams(
            collective_id=0, has_side_effects=True, vmem_limit_bytes=42 * 2**20
        ),
    )(
        control.reshape(rows, cols), filters, weights[0],
        jnp.transpose(vertical, (0, 2, 1)), balance,
    )
    out = pl.pallas_call(
        write_kernel,
        out_shape=jax.ShapeDtypeStruct((levels, rows, cols), jnp.bfloat16),
        in_specs=[pl.BlockSpec(memory_space=pl.ANY)],
        out_specs=pl.BlockSpec(memory_space=pl.ANY),
        scratch_shapes=[dma((levels, PARTS))],
        compiler_params=pltpu.CompilerParams(vmem_limit_bytes=2**20),
    )(pltpu.with_memory_space_constraint(out, pltpu.VMEM))
    return out.reshape(members, 1, levels, rows, cols)


def solution(mesh):
    in_specs = (P(None, "var", "mode", None, None), P(), P("var", None, None, None), P(), P())
    out_specs = P(None, "var", "mode", None, None)
    nmode, nvar = mesh.shape["mode"], mesh.shape["var"]

    def run(control, filters, weights, vertical, balance):
        members, _, modes, rows, cols = control.shape
        levels = vertical.shape[1] // nmode
        gather = members == 1 and modes == nmode and nmode == LINE * PAIRS and nvar == 4
        gather = gather and rows % (8 * STRIP) == 0 and levels > 2 * filters.shape[0]
        gather = gather and (2 * modes + levels) * rows * cols * 2 <= 48 * 2**20
        body = per_device_gather if gather else per_device_exchange
        return jax.shard_map(
            body, mesh=mesh, in_specs=in_specs, out_specs=out_specs, check_vma=False
        )(control, filters, weights, vertical, balance)

    return run
```
